32 devices in a mesh: groups: 2 (over y), seq: 8 (over z, x), heads: 2 (over core).
Axes of the slice: x: 2, y: 2, z: 4, core: 2. Of those that a mesh axis runs over, the one named last changes fastest.
Arguments:
- queries: bfloat16 [4096, 16, 128], P(('groups', 'seq'), 'heads'), parts along dimension 0, may hold values from -20 to 20
- keys: bfloat16 [4096, 16, 128], P(('groups', 'seq'), 'heads'), parts along dimension 0, may hold values from -18 to 18
- values: bfloat16 [4096, 16, 128], P(('groups', 'seq'), 'heads'), parts along dimension 0, may hold values from -6 to 6
- out_grad: bfloat16 [4096, 16, 128], P(('groups', 'seq'), 'heads'), parts along dimension 0, may hold values from -6 to 6
- spans: int32 [3, 4096], P(None, ('groups', 'seq')), parts along dimension 1, may hold values from 0 to 2048, as said below
Outputs:
- attended: bfloat16 [4096, 16, 128], P(('groups', 'seq'), 'heads'), parts along dimension 0
- query_grad: bfloat16 [4096, 16, 128], P(('groups', 'seq'), 'heads'), parts along dimension 0
- key_grad: bfloat16 [4096, 16, 128], P(('groups', 'seq'), 'heads'), parts along dimension 0
- value_grad: bfloat16 [4096, 16, 128], P(('groups', 'seq'), 'heads'), parts along dimension 0
The draws below stay inside these ranges and needn't reach their ends.
There are 2 independent parts, one for each index of `groups`. The reference program is written for one: setup_inputs(seed, part) draws one part's arguments, and reference() takes and returns one part's arrays. A program takes and returns all parts, laid end to end along the dimension named above; each array names one. Nothing has to cross between parts.
Inputs may be any that keep to these rules, and one draw needn't show every extreme that they name: Triples lie end to end from position 0; for each token spans[0] <= position, spans[0] < spans[1] <= spans[2], and all tokens of a triple share the three values. A triple holds at most 512 tokens, and one holds exactly 512. The triple that holds the last token has spans[2] = 2048.
All inputs are finite; a program needn't handle non-finite values.
Results may differ from the reference program's by a relative error of at most 0.022.
Values may be sent and summed in bfloat16 or wider, within the bound.
No kernel may reach another device: no remote copies, remote signals or barrier semaphores. Data moves between devices by JAX's collectives and lax.ppermute only.
A program may use at most 64 MiB of HBM per device.

```python
import math
import jax
import jax.numpy as jnp
from jax import lax

HEADS = 16
HD = 128
REACH = 2
TOK_DEV = 256
SEQ = 2048
TRIPLE_MAX = 512


def joint_fields(key):
    base = jax.random.fold_in(key, 101)
    seed_query, seed_keys = jax.random.split(base, 2)
    field_shape = (SEQ, HEADS, HD)
    query_field = jnp.clip(jax.random.normal(seed_query, field_shape, jnp.float32), -6.0, 6.0)
    key_field = jnp.clip(jax.random.normal(seed_keys, field_shape, jnp.float32), -6.0, 6.0)
    return (query_field, key_field)


def draw_queries(key, part):
    return joint_fields(key)[0].astype(jnp.bfloat16)


def draw_keys(key, part):
    return joint_fields(key)[1].astype(jnp.bfloat16)


def draw_spans(key, part):
    base = jax.random.fold_in(key, 202)
    seed_length, seed_prompt, seed_chosen, seed_longest = jax.random.split(base, 4)
    shortest = TRIPLE_MAX // 4
    triple_count = SEQ // shortest + 2
    lengths = jax.random.randint(seed_length, (triple_count,), shortest, TRIPLE_MAX + 1)
    longest = jax.random.randint(seed_longest, (), 0, max(SEQ // TRIPLE_MAX, 1))
    triple_index = jnp.arange(triple_count)
    lengths = jnp.where(triple_index == longest, TRIPLE_MAX, lengths)
    triple_ends = jnp.cumsum(lengths)
    triple_starts = triple_ends - lengths
    prompt = 1 + (lengths - 3) * jax.random.randint(seed_prompt, (triple_count,), 20, 51) // 100
    chosen = 1 + (lengths - 2 - prompt) * jax.random.randint(seed_chosen, (triple_count,), 30, 71) // 100
    positions = jnp.arange(SEQ)
    owner = jnp.sum((triple_ends[None, :] <= positions[:, None]).astype(jnp.int32), axis=1)
    final_owner = owner[SEQ - 1]
    triple_first = triple_starts[owner]
    chosen_first = jnp.minimum(triple_first + prompt[owner], SEQ)
    rejected_first = jnp.where(owner == final_owner, SEQ, jnp.minimum(chosen_first + chosen[owner], SEQ))
    return jnp.stack((triple_first, chosen_first, rejected_first)).astype(jnp.int32)


def steps_of(own_key, extent, cuts, low, high):
    def one(axis_at, blocks):
        steps = jax.random.uniform(jax.random.fold_in(jax.random.fold_in(own_key, 6), axis_at), (blocks,), jnp.float32, low / len(cuts), high / len(cuts))
        return jnp.repeat(jnp.exp(steps), extent[axis_at] // blocks).reshape((-1,) + (1,) * (len(extent) - axis_at - 1))

    factor_of = one(*cuts[0])
    for cut in cuts[1:]:
        factor_of = factor_of * one(*cut)
    return factor_of


def gaussian(key, dims, spread, reach, pieces=(), kind=jnp.bfloat16):
    loudness = steps_of(key, dims, pieces, -0.22, 0.18) if pieces else 1.0
    values = jax.random.normal(key, dims, jnp.float32) * spread * loudness
    return jnp.minimum(jnp.maximum(values, -reach), reach).astype(kind)


def setup_inputs(seed: int = 0, part: int = 0) -> dict:
    splits = jax.random.split(jax.random.key(seed), 6)
    own_keys = jax.random.split(jax.random.fold_in(splits[5], part), 6)
    return {
        "queries": draw_queries(jax.random.fold_in(jax.random.fold_in(splits[5], part), 71), part),
        "keys": draw_keys(jax.random.fold_in(jax.random.fold_in(splits[5], part), 71), part),
        "values": gaussian(own_keys[2], (SEQ, HEADS, HD), 1.0, 6.0, ((0, 8), (1, 2))),
        "out_grad": gaussian(own_keys[3], (SEQ, HEADS, HD), 1.0, 6.0, ((0, 8), (1, 2))),
        "spans": draw_spans(jax.random.fold_in(jax.random.fold_in(splits[5], part), 71), part),
    }


NEG = -1e+30

def rounded(tensor):
    return lax.optimization_barrier(tensor.astype(jnp.bfloat16)).astype(jnp.float32)

def reference(queries, keys, values, out_grad, spans):
    score_scale = 1.0 / math.sqrt(HD)
    reach_rows = REACH * TOK_DEV
    window = reach_rows + TOK_DEV
    padding = ((reach_rows, 0), (0, 0), (0, 0))
    keys_padded = jnp.pad(keys, padding)
    values_padded = jnp.pad(values, padding)
    offsets = jnp.arange(TOK_DEV, dtype=jnp.int32)
    window_offsets = jnp.arange(window, dtype=jnp.int32)
    block_count = SEQ // TOK_DEV

    def step_block(accumulated, block_index):
        anchor = (block_index * TOK_DEV).astype(jnp.int32)
        query_pos = anchor + offsets
        key_pos = anchor - reach_rows + window_offsets
        starts = lax.dynamic_slice_in_dim(spans[0], anchor, TOK_DEV)
        chosen = lax.dynamic_slice_in_dim(spans[1], anchor, TOK_DEV)
        rejected = lax.dynamic_slice_in_dim(spans[2], anchor, TOK_DEV)
        allowed = (key_pos[None, :] >= starts[:, None]) & (key_pos[None, :] <= query_pos[:, None])
        crossed = (query_pos >= rejected)[:, None] & (key_pos[None, :] >= chosen[:, None]) & (key_pos[None, :] < rejected[:, None])
        visible = allowed & jnp.logical_not(crossed)
        query_block = lax.dynamic_slice_in_dim(queries, anchor, TOK_DEV).astype(jnp.float32)
        grad_block = lax.dynamic_slice_in_dim(out_grad, anchor, TOK_DEV).astype(jnp.float32)
        key_block = lax.dynamic_slice_in_dim(keys_padded, anchor, window).astype(jnp.float32)
        value_block = lax.dynamic_slice_in_dim(values_padded, anchor, window).astype(jnp.float32)
        scores = jnp.einsum('qhd,khd->hqk', query_block, key_block) * score_scale
        scores = jnp.where(visible[None], scores, NEG)
        row_max = lax.optimization_barrier(jnp.max(scores, axis=-1))
        weights = jnp.exp(scores - row_max[..., None])
        row_sum = lax.optimization_barrier(jnp.sum(weights, axis=-1))
        mixed = jnp.einsum('hqk,khd->qhd', rounded(weights), value_block)
        attended = (mixed / row_sum.T[:, :, None]).astype(jnp.bfloat16)
        log_total = row_max + jnp.log(row_sum)
        probs = jnp.exp(scores - log_total[..., None])
        delta = lax.optimization_barrier(jnp.sum(grad_block * attended.astype(jnp.float32), axis=-1)).T
        value_part = jnp.einsum('hqk,qhd->khd', rounded(probs), grad_block)
        prob_grad = jnp.einsum('qhd,khd->hqk', grad_block, value_block)
        score_grad = rounded(probs * (prob_grad - delta[..., None]))
        query_grad = (jnp.einsum('hqk,khd->qhd', score_grad, key_block) * score_scale).astype(jnp.bfloat16)
        key_part = jnp.einsum('hqk,qhd->khd', score_grad, query_block) * score_scale
        current = lax.dynamic_slice_in_dim(accumulated, anchor, window, axis=1)
        updated = current + jnp.stack((key_part, value_part))
        accumulated = lax.dynamic_update_slice_in_dim(accumulated, updated, anchor, axis=1)
        return (accumulated, (attended, query_grad))
    initial = jnp.zeros((2, SEQ + reach_rows, HEADS, HD), jnp.float32)
    accumulated, (attended, query_grad) = lax.scan(step_block, initial, jnp.arange(block_count, dtype=jnp.int32))
    attended = attended.reshape(SEQ, HEADS, HD)
    query_grad = query_grad.reshape(SEQ, HEADS, HD)
    key_grad = accumulated[0, reach_rows:].astype(jnp.bfloat16)
    value_grad = accumulated[1, reach_rows:].astype(jnp.bfloat16)
    return (attended, query_grad, key_grad, value_grad)
```

```python
import functools
import math

import jax
import jax.numpy as jnp
from jax import lax
from jax.experimental import pallas as pl
from jax.experimental.pallas import tpu as pltpu
from jax.sharding import PartitionSpec as P

NEG = -1e30
BF = jnp.bfloat16
F32 = jnp.float32
LOG2E = math.log2(math.e)


def nt(a, b):
    return lax.dot_general(a, b, (((1,), (1,)), ((), ())), preferred_element_type=F32)


def nn(a, b):
    return jnp.dot(a, b, preferred_element_type=F32)


def cost(flops, nbytes):
    return pl.CostEstimate(flops=int(flops), bytes_accessed=int(nbytes), transcendentals=0)


def prep_kernel(seq_ref, q_ref, k_ref, v_ref, g_ref, kv0, kv1, qd0, qd1, e0):
    half = kv0.shape[1]
    even = seq_ref[0] % 2 == 0
    for slot, (own, queried) in enumerate(((k_ref, q_ref), (v_ref, g_ref))):
        a = pltpu.einshape("mhd->hmd", own[...])
        b = pltpu.einshape("mhd->hmd", queried[...])
        kv0[slot] = a[:half]
        kv1[slot] = a[half:]
        qd0[slot] = b[:half]
        qd1[slot] = b[half:]
        e0[slot] = jnp.where(even, a[:half], b[:half])


def prep(seq, q, k, v, g, steps=4):
    rows, heads, size = q.shape
    block = rows // steps
    part = jax.ShapeDtypeStruct((2, heads // 2, rows, size), q.dtype)
    return pl.pallas_call(
        prep_kernel,
        out_shape=(part,) * 5,
        grid_spec=pltpu.PrefetchScalarGridSpec(
            num_scalar_prefetch=1,
            grid=(steps,),
            in_specs=[pl.BlockSpec((block, heads, size), lambda i, s: (i, 0, 0))] * 4,
            out_specs=[pl.BlockSpec((2, heads // 2, block, size), lambda i, s: (0, 0, i, 0))] * 5,
        ),
        cost_estimate=cost(0, 9 * q.size * 2),
        name="prep",
    )(seq, q, k, v, g)


def query_kernel(seq_ref, sp_ref, kv_ref, qd_ref, far_ref, odd_ref, even_ref,
                 att_ref, dq_ref, st_ref, bias, cols):
    heads, rows, size = kv_ref.shape[1:]
    seq = seq_ref[0]
    anchor = seq * rows
    odd = seq % 2 == 1
    scale = 1.0 / math.sqrt(size)
    sp = jnp.concatenate([sp_ref[...].astype(F32), jnp.zeros((5, rows), F32)], axis=0)
    spt = sp.T
    start, chosen, rejected = spt[:, 0:1], spt[:, 1:2], spt[:, 2:3]
    shape = (rows, rows)
    qpos = (anchor + lax.broadcasted_iota(jnp.int32, shape, 0)).astype(F32)
    qrej = qpos >= rejected
    for t in range(3):
        kpos = (anchor - t * rows + lax.broadcasted_iota(jnp.int32, shape, 1)).astype(F32)
        ok = (kpos >= start) & (kpos <= qpos)
        ok = ok & jnp.logical_not(qrej & (kpos >= chosen) & (kpos < rejected))
        bias[t] = jnp.where(ok, 0.0, NEG)
    lane = lax.broadcasted_iota(jnp.int32, (rows, 128), 1)
    stat = jnp.zeros((rows, 128), F32)
    for h in range(heads):
        q = qd_ref[0, h]
        g = qd_ref[1, h]
        ks = (kv_ref[0, h], jnp.where(odd, odd_ref[0, h], even_ref[0, h]), far_ref[0, h])
        vs = (kv_ref[1, h], jnp.where(odd, odd_ref[1, h], even_ref[1, h]), far_ref[1, h])
        s = [nt(q, ks[t]) * (scale * LOG2E) + bias[t] for t in range(3)]
        top = functools.reduce(jnp.maximum, [jnp.max(x, axis=1, keepdims=True) for x in s])
        p = [jnp.exp2(x - top) for x in s]
        total = sum(jnp.sum(x, axis=1, keepdims=True) for x in p)
        inv = 1.0 / total
        mixed = sum(nn(p[t].astype(BF), vs[t]) for t in range(3))
        att = (mixed * inv).astype(BF)
        delta = jnp.sum(g.astype(F32) * att.astype(F32), axis=1, keepdims=True)
        ds = [(p[t] * inv * (nt(g, vs[t]) - delta)).astype(BF) for t in range(3)]
        dq = sum(nn(ds[t], ks[t]) for t in range(3)) * scale
        att_ref[h] = att
        dq_ref[h] = dq.astype(BF)
        stat = jnp.where(lane == h, top + jnp.log2(total), stat)
        stat = jnp.where(lane == heads + h, delta, stat)
    row = stat.T[: 2 * heads]
    st_ref[0] = row
    low = sp_ref[0:1, :]
    is_lse = lax.broadcasted_iota(jnp.int32, row.shape, 0) < heads
    for t in (1, 2):
        reaches = low < anchor - (t - 1) * rows
        st_ref[t] = jnp.where(is_lse & jnp.logical_not(reaches), -NEG, row)


def query_side(seq, spans, kv, qd, far, odd, even):
    _, heads, rows, size = kv.shape
    out = jax.ShapeDtypeStruct((heads, rows, size), BF)
    vm = pl.BlockSpec(memory_space=pltpu.VMEM)
    return pl.pallas_call(
        query_kernel,
        out_shape=(out, out, jax.ShapeDtypeStruct((3, 2 * heads, rows), F32)),
        in_specs=[pl.BlockSpec(memory_space=pltpu.SMEM)] + [vm] * 6,
        out_specs=[vm] * 3,
        scratch_shapes=[pltpu.VMEM((3, rows, rows), F32), pltpu.VMEM((rows, 128), F32)],
        cost_estimate=cost(heads * 3 * 4 * 2 * rows * rows * size * 4, 6 * kv.size * 2),
        name="query_side",
    )(seq, spans, kv, qd, far, odd, even)


def key_tile(k, v, q, g, lse, delta, bias, factor):
    s = nt(k, q) * factor + bias
    p = jnp.exp2(s - lse)
    dv = nn(p.astype(BF), g)
    ds = (p * (nt(v, g) - delta)).astype(BF)
    return nn(ds, q), dv


def own_bias(sp_ref, anchor, rows):
    shape = (rows, rows)
    kpos = anchor + lax.broadcasted_iota(jnp.int32, shape, 0)
    qpos = anchor + lax.broadcasted_iota(jnp.int32, shape, 1)
    start, chosen, rejected = sp_ref[0:1, :], sp_ref[1:2, :], sp_ref[2:3, :]
    ok = (kpos >= start) & (kpos <= qpos)
    ok = ok & jnp.logical_not((qpos >= rejected) & (kpos >= chosen) & (kpos < rejected))
    return jnp.where(ok, 0.0, NEG)


def later_bias(sp_ref, anchor, rows, t):
    shape = (rows, rows)
    kpos = anchor + lax.broadcasted_iota(jnp.int32, shape, 0)
    qpos = anchor + t * rows + lax.broadcasted_iota(jnp.int32, shape, 1)
    last = rows - 1
    start = sp_ref[0:1, last : last + 1]
    chosen = sp_ref[1:2, last : last + 1]
    rejected = sp_ref[2:3, last : last + 1]
    ok = kpos >= start
    ok = ok & jnp.logical_not((qpos >= rejected) & (kpos >= chosen) & (kpos < rejected))
    return jnp.where(ok, 0.0, NEG)


def early_kernel(seq_ref, sp_ref, kv_ref, qd_ref, far_ref, st_ref, st2_ref, acc_ref, bias):
    heads, rows, size = kv_ref.shape[1:]
    anchor = seq_ref[0] * rows
    factor = LOG2E / math.sqrt(size)
    bias[0] = own_bias(sp_ref, anchor, rows)
    bias[1] = later_bias(sp_ref, anchor, rows, 2)
    for h in range(heads):
        k = kv_ref[0, h]
        v = kv_ref[1, h]
        dk, dv = key_tile(k, v, qd_ref[0, h], qd_ref[1, h], st_ref[0, h : h + 1],
                          st_ref[0, heads + h : heads + h + 1], bias[0], factor)
        dk2, dv2 = key_tile(k, v, far_ref[0, h], far_ref[1, h], st2_ref[h : h + 1],
                            st2_ref[heads + h : heads + h + 1], bias[1], factor)
        acc_ref[0, h] = dk + dk2
        acc_ref[1, h] = dv + dv2


def early(seq, spans, kv, qd, far, st, st2):
    _, heads, rows, size = kv.shape
    vm = pl.BlockSpec(memory_space=pltpu.VMEM)
    return pl.pallas_call(
        early_kernel,
        out_shape=jax.ShapeDtypeStruct((2, heads, rows, size), F32),
        in_specs=[pl.BlockSpec(memory_space=pltpu.SMEM)] + [vm] * 6,
        out_specs=vm,
        scratch_shapes=[pltpu.VMEM((2, rows, rows), F32)],
        cost_estimate=cost(heads * 2 * 4 * 2 * rows * rows * size * 4, 5 * kv.size * 2),
        name="early",
    )(seq, spans, kv, qd, far, st, st2)


def late_kernel(seq_ref, sp_ref, kv_ref, odd_ref, even_ref, st1_ref, acc_ref, out_ref, bias):
    heads, rows, size = kv_ref.shape[1:]
    seq = seq_ref[0]
    anchor = seq * rows
    odd = seq % 2 == 1
    scale = 1.0 / math.sqrt(size)
    bias[...] = later_bias(sp_ref, anchor, rows, 1)
    for h in range(heads):
        q = jnp.where(odd, odd_ref[0, h], even_ref[0, h])
        g = jnp.where(odd, odd_ref[1, h], even_ref[1, h])
        dk, dv = key_tile(kv_ref[0, h], kv_ref[1, h], q, g, st1_ref[h : h + 1],
                          st1_ref[heads + h : heads + h + 1], bias[...], scale * LOG2E)
        out_ref[0, h] = ((acc_ref[0, h] + dk) * scale).astype(BF)
        out_ref[1, h] = (acc_ref[1, h] + dv).astype(BF)


def late(seq, spans, kv, odd, even, st1, acc):
    _, heads, rows, size = kv.shape
    vm = pl.BlockSpec(memory_space=pltpu.VMEM)
    return pl.pallas_call(
        late_kernel,
        out_shape=jax.ShapeDtypeStruct((2, heads, rows, size), BF),
        in_specs=[pl.BlockSpec(memory_space=pltpu.SMEM)] + [vm] * 6,
        out_specs=vm,
        scratch_shapes=[pltpu.VMEM((rows, rows), F32)],
        cost_estimate=cost(heads * 4 * 2 * rows * rows * size * 4, 6 * kv.size * 2),
        name="late",
    )(seq, spans, kv, odd, even, st1, acc)


def last_kernel(seq_ref, sp_ref, kv_ref, new_ref, st1_ref, acc_ref, first_ref,
                dk_ref, dv_ref, bias, sums):
    heads, rows, size = kv_ref.shape[1:]
    anchor = seq_ref[0] * rows
    scale = 1.0 / math.sqrt(size)
    bias[...] = later_bias(sp_ref, anchor, rows, 1)
    for h in range(heads):
        dk, dv = key_tile(kv_ref[0, h], kv_ref[1, h], new_ref[0, h], new_ref[1, h],
                          st1_ref[h : h + 1], st1_ref[heads + h : heads + h + 1], bias[...],
                          scale * LOG2E)
        sums[0, heads + h] = ((acc_ref[0, h] + dk) * scale).astype(BF)
        sums[1, heads + h] = (acc_ref[1, h] + dv).astype(BF)
    for slot, ref in enumerate((dk_ref, dv_ref)):
        sums[slot, :heads] = first_ref[slot]
        ref[...] = pltpu.einshape("hmd->mhd", sums[slot])


def last(seq, spans, kv, new, st1, acc, first):
    _, heads, rows, size = kv.shape
    vm = pl.BlockSpec(memory_space=pltpu.VMEM)
    out = jax.ShapeDtypeStruct((rows, 2 * heads, size), BF)
    return pl.pallas_call(
        last_kernel,
        out_shape=(out, out),
        in_specs=[pl.BlockSpec(memory_space=pltpu.SMEM)] + [vm] * 6,
        out_specs=[vm] * 2,
        scratch_shapes=[pltpu.VMEM((rows, rows), F32), pltpu.VMEM((2, 2 * heads, rows, size), BF)],
        cost_estimate=cost(heads * 4 * 2 * rows * rows * size * 4, 8 * kv.size * 2),
        name="last",
    )(seq, spans, kv, new, st1, acc, first)


def join_kernel(a0, a1, b0, b1, a_ref, b_ref):
    a_ref[...] = pltpu.einshape("hmd->mhd", jnp.concatenate([a0[...], a1[...]], axis=0))
    b_ref[...] = pltpu.einshape("hmd->mhd", jnp.concatenate([b0[...], b1[...]], axis=0))


def join(a0, a1, b0, b1):
    heads, rows, size = a0.shape
    out = jax.ShapeDtypeStruct((rows, 2 * heads, size), BF)
    vm = pl.BlockSpec(memory_space=pltpu.VMEM)
    return pl.pallas_call(
        join_kernel,
        out_shape=(out, out),
        in_specs=[vm] * 4,
        out_specs=[vm] * 2,
        cost_estimate=cost(0, 8 * a0.size * 2),
        name="join",
    )(a0, a1, b0, b1)


def per_device(queries, keys, values, out_grad, spans):
    count = lax.axis_size("seq")
    index = lax.axis_index("seq")
    seq = index.astype(jnp.int32).reshape(1)
    even = index % 2 == 0

    def move(value, by):
        pairs = [(i, i + by) for i in range(count) if 0 <= i + by < count]
        return lax.ppermute(value, "seq", pairs)

    def swap(value):
        return lax.ppermute(value, "seq", [(i, i ^ 1) for i in range(count) if (i ^ 1) < count])

    kv0, kv1, qd0, qd1, e0 = prep(seq, queries, keys, values, out_grad)
    a0 = move(kv0, 2)
    x0 = swap(e0)
    c0 = move(qd0, -2)
    a1 = move(kv1, 2)
    x1 = swap(jnp.where(even, kv1, a0))
    c1 = move(qd1, -2)
    x2 = swap(jnp.where(even, c0, a1))
    x3 = swap(jnp.where(even, c1, qd1))
    att0, dq0, st0 = query_side(seq, spans, kv0, qd0, a0, x0, x1)
    n0 = move(st0[1], -1)
    f0 = move(st0[2], -2)
    att1, dq1, st1 = query_side(seq, spans, kv1, qd1, a1, x1, x2)
    n1 = move(st1[1], -1)
    f1 = move(st1[2], -2)
    acc0 = early(seq, spans, kv0, qd0, c0, st0, f0)
    first = late(seq, spans, kv0, x2, x0, n0, acc0)
    acc1 = early(seq, spans, kv1, qd1, c1, st1, f1)
    attended, query_grad = join(att0, att1, dq0, dq1)
    key_grad, value_grad = last(seq, spans, kv1, x3, n1, acc1, first)
    return (attended, query_grad, key_grad, value_grad)


def solution(mesh):
    rows = P(("groups", "seq"), "heads", None)
    in_specs = (rows, rows, rows, rows, P(None, ("groups", "seq")))
    return jax.shard_map(
        per_device, mesh=mesh, in_specs=in_specs, out_specs=(rows,) * 4, check_vma=False
    )
```
